32 devices in a mesh: tm: 8 (over y, x, core), panel: 4 (over z).
Axes of the slice: x: 2, y: 2, z: 4, core: 2. Of those that a mesh axis runs over, the one named last changes fastest.
Arguments:
- series: float32 [48, 2048], P(None, 'tm'), may hold values from -20 to 20, as said below
- start_block: float32 [18432, 64], P(('tm', 'panel')), may hold values from -6 to 6
Outputs:
- covariance: float32 [18432, 18432], P(('tm', 'panel'))
- basis: float32 [7, 18432, 64], P(None, ('tm', 'panel'))
- diag_blocks: float32 [6, 64, 64], replicated
- off_blocks: float32 [7, 64, 64], replicated
The draws below stay inside these ranges and needn't reach their ends.
Inputs may be any that keep to these rules, and one draw needn't show every extreme that they name: `series`: each channel has its own scale.
All inputs are finite; a program needn't handle non-finite values.
Results may differ from the reference program's by a relative error of at most 0.0003.
Values sent between devices are 32-bit elements; how exact they have to be, the bound alone decides.
No kernel may reach another device: no remote copies, remote signals or barrier semaphores. Data moves between devices by JAX's collectives and lax.ppermute only.
A program may use at most 192 MiB of HBM per device.

```python
import math
import jax
import jax.numpy as jnp
from jax import lax

L = 48
M = 384
B = 64
ITERS = 6
NT = 2048
LM = 18432


def draw_series(key, part):
    scale_key = jax.random.fold_in(key, 11)
    noise_key = jax.random.fold_in(key, 12)
    scales = jnp.exp(jax.random.uniform(scale_key, (L, 1), jnp.float32, math.log(0.3), math.log(3.0)))
    noise = jnp.clip(jax.random.normal(noise_key, (L, NT), jnp.float32), -6.0, 6.0)
    return (scales * noise).astype(jnp.float32)


def block_levels(rng, dims, split, low, top_value):
    def one(axis_at, blocks):
        draws = jax.random.uniform(jax.random.fold_in(jax.random.fold_in(rng, 6), axis_at), (blocks,), jnp.float32, low / len(split), top_value / len(split))
        return jnp.repeat(jnp.exp(draws), dims[axis_at] // blocks).reshape((-1,) + (1,) * (len(dims) - axis_at - 1))

    factor_of = one(*split[0])
    for cut in split[1:]:
        factor_of = factor_of * one(*cut)
    return factor_of


def centred(rng, shape, scale, limit, split=(), kind=jnp.bfloat16):
    array = scale * jax.random.normal(rng, shape, jnp.float32)
    if split:
        array = array * block_levels(rng, shape, split, -0.22, 0.18)
    return jnp.clip(array, -limit, limit).astype(kind)


def setup_inputs(seed: int = 0) -> dict:
    seeds = jax.random.split(jax.random.key(seed), 3)
    return {
        "series": draw_series(jax.random.fold_in(seeds[2], 71), 0),
        "start_block": centred(seeds[1], (LM, B), 1.0, 6.0, ((0, 32),), jnp.float32),
    }


exact_precision = lax.Precision.HIGHEST

def lower_factor(gram_matrix):
    return jnp.linalg.cholesky(gram_matrix)

def reference(series, start_block):
    padded = jnp.concatenate([series, jnp.zeros((L, M), jnp.float32)], axis=1)

    def one_lag(lag_index):
        shifted = lax.dynamic_slice(padded, (jnp.int32(0), lag_index.astype(jnp.int32)), (L, NT))
        return jnp.dot(series.astype(jnp.float32), shifted.T.astype(jnp.float32), precision=exact_precision, preferred_element_type=jnp.float32)
    lag_sums = lax.map(one_lag, jnp.arange(M, dtype=jnp.int32))
    lag_sums = jnp.transpose(lag_sums, (1, 0, 2))
    counts = (NT - jnp.arange(M)).astype(jnp.float32)
    normed = lag_sums / counts[None, :, None]
    two_sided = jnp.concatenate([jnp.transpose(normed, (2, 1, 0))[:, :0:-1, :], normed], axis=1)

    def one_row(lag_index):
        window = lax.dynamic_slice(two_sided, (jnp.int32(0), (M - 1 - lag_index).astype(jnp.int32), jnp.int32(0)), (L, M, L))
        return window.reshape(L, M * L)
    covariance = lax.map(one_row, jnp.arange(M, dtype=jnp.int32)).reshape(M * L, M * L)
    factor = lower_factor(jnp.dot(start_block.T.astype(jnp.float32), start_block.astype(jnp.float32), precision=exact_precision, preferred_element_type=jnp.float32))
    current = jax.scipy.linalg.solve_triangular(factor, start_block.T, lower=True).T
    previous = jnp.zeros_like(current)
    upper = factor.T
    basis_list = [current]
    diagonal_list = []
    upper_list = [upper]
    for iteration in range(ITERS):
        work = jnp.dot(covariance.astype(jnp.float32), current.astype(jnp.float32), precision=exact_precision, preferred_element_type=jnp.float32)
        if iteration > 0:
            work = work - jnp.dot(previous.astype(jnp.float32), upper.T.astype(jnp.float32), precision=exact_precision, preferred_element_type=jnp.float32)
        diagonal = jnp.dot(current.T.astype(jnp.float32), work.astype(jnp.float32), precision=exact_precision, preferred_element_type=jnp.float32)
        work = work - jnp.dot(current.astype(jnp.float32), diagonal.astype(jnp.float32), precision=exact_precision, preferred_element_type=jnp.float32)
        factor = lower_factor(jnp.dot(work.T.astype(jnp.float32), work.astype(jnp.float32), precision=exact_precision, preferred_element_type=jnp.float32))
        upper = factor.T
        previous = current
        current = jax.scipy.linalg.solve_triangular(factor, work.T, lower=True).T
        basis_list.append(current)
        diagonal_list.append(diagonal)
        upper_list.append(upper)
    return (covariance, jnp.stack(basis_list), jnp.stack(diagonal_list), jnp.stack(upper_list))
```

```python
import jax
import jax.numpy as jnp
from jax import lax
from jax.experimental import pallas as pl
from jax.experimental.pallas import tpu as pltpu
from jax.sharding import PartitionSpec as P

M = 384
ITERS = 6
GROUP = 16
K_STEP = 1280
CHUNK = 1536

exact_precision = lax.Precision.HIGHEST
f32 = jnp.float32
bf16 = jnp.bfloat16


def shifted_around(block, axis):
    size = lax.axis_size(axis)
    received = [block]
    for distance in range(1, size):
        route = [(i, (i + distance) % size) for i in range(size)]
        received.append(lax.ppermute(block, axis, route))
    return received


def exact_dot(left, right, dims=((1,), (0,))):
    return lax.dot_general(
        left, right, (dims, ((), ())), precision=exact_precision, preferred_element_type=f32
    )


def fast_dot(left, right):
    return jnp.dot(left, right, preferred_element_type=f32)


def lag_kernel(both_ref, high_ref, low_ref, count_ref, window_ref, split_ref):
    channels = both_ref.shape[0] // 2
    days = both_ref.shape[1]
    width = high_ref.shape[1]
    day_step = min(days, 2048)

    def group(g, carry):
        total = jnp.zeros((channels, width), f32)
        for first in range(0, days, day_step):
            row = pl.multiple_of(g * GROUP + first, GROUP)
            left = both_ref[:, first : first + day_step]
            high = fast_dot(left, high_ref[pl.ds(row, day_step), :])
            low = fast_dot(left[:channels], low_ref[pl.ds(row, day_step), :])
            total = total + (high[:channels] + (high[channels:] + low))
        lanes = pl.ds(pl.multiple_of(g * width, 128), width)
        value = total / count_ref[:, lanes]
        window_ref[:, lanes] = value
        upper_half = value.astype(bf16)
        split_ref[:channels, lanes] = upper_half
        split_ref[channels:, lanes] = (value - upper_half.astype(f32)).astype(bf16)
        return carry

    lax.fori_loop(0, window_ref.shape[1] // width, group, 0)


def split_halves(values):
    high = lax.reduce_precision(values, 8, 7)
    return high.astype(bf16), (values - high).astype(bf16)


def lag_window(series, block_index, lags_here):
    channels, days = series.shape
    groups = -(-(M + lags_here) // GROUP)
    rows = days + groups * GROUP
    width = GROUP * channels
    padded = jnp.pad(series.T, ((M, rows + GROUP - days), (0, 0)))
    base = M - (lags_here - 1) - block_index * lags_here
    placed = lax.dynamic_slice(padded, (base, jnp.int32(0)), (rows + GROUP, channels))
    high, low = split_halves(placed)
    high = jnp.concatenate([high[r : r + rows] for r in range(GROUP)], axis=1)
    low = jnp.concatenate([low[r : r + rows] for r in range(GROUP)], axis=1)
    both = jnp.concatenate(split_halves(series), axis=0)
    lag = jnp.arange(groups * GROUP) - (lags_here - 1) - block_index * lags_here
    count = jnp.repeat((days - jnp.abs(lag)).astype(f32), channels)[None, :]
    length = groups * width
    return pl.pallas_call(
        lag_kernel,
        out_shape=(
            jax.ShapeDtypeStruct((channels, length), f32),
            jax.ShapeDtypeStruct((2 * channels, length), bf16),
        ),
        name="lag_window",
    )(both, high, low, count)


def covariance_kernel(window_ref, out_ref):
    channels, length = out_ref.shape
    lags_here = pl.num_programs(0)
    for shift in range(M):
        if shift >= covariance_kernel.lags:
            break

        @pl.when(pl.program_id(0) == lags_here - 1 - shift)
        def _(shift=shift):
            first = shift * channels
            aligned = first // 128 * 128
            rest = first - aligned

            def chunk(c, carry):
                source = pl.multiple_of(aligned + c * CHUNK, 128)
                piece = window_ref[:, pl.ds(source, CHUNK + 128)]
                out_ref[:, pl.ds(pl.multiple_of(c * CHUNK, 128), CHUNK)] = piece[:, rest : rest + CHUNK]
                return carry

            lax.fori_loop(0, length // CHUNK, chunk, 0)


def covariance_rows(window, lags_here):
    channels = window.shape[0]
    length = M * channels
    covariance_kernel.lags = lags_here
    return pl.pallas_call(
        covariance_kernel,
        grid=(lags_here,),
        in_specs=[pl.BlockSpec(window.shape, lambda i: (0, 0))],
        out_specs=pl.BlockSpec((channels, length), lambda i: (i, 0)),
        out_shape=jax.ShapeDtypeStruct((lags_here * channels, length), f32),
        name="covariance_rows",
    )(window)


def factor_and_inverse(gram, result_ref):
    n = gram.shape[0]
    row_id = lax.broadcasted_iota(jnp.int32, (n, n), 0)
    col_id = lax.broadcasted_iota(jnp.int32, (n, n), 1)
    rest = jnp.concatenate([gram, (row_id == col_id).astype(f32)], axis=1)
    for k in range(n):
        at = k % 8
        if k and at == 0:
            rest = rest[8:]
        row = rest[at : at + 1]
        pivot = row[:, k : k + 1]
        root = lax.rsqrt(pivot)
        root = root * (1.5 - 0.5 * pivot * root * root)
        row = row * root
        result_ref[k : k + 1, :] = row
        below = lax.broadcasted_iota(jnp.int32, (rest.shape[0], 1), 0) > at
        column = jnp.where(below, rest[:, k : k + 1] * root, 0.0)
        rest = rest - column * row
    upper = jnp.where(col_id >= row_id, result_ref[:, :n], 0.0)
    return upper, result_ref[:, n:]


def orthogonalize(gram, work, current, result_ref):
    n = work.shape[1]
    diagonal = gram[:n, n:]
    weighted = exact_dot(gram[:n, :n], diagonal) - 2.0 * diagonal
    reduced = gram[n:, n:] + exact_dot(diagonal, weighted, ((0,), (0,)))
    upper, inverse = factor_and_inverse(reduced, result_ref)
    cleaned = work - exact_dot(current, diagonal)
    return diagonal, upper, inverse, exact_dot(cleaned, inverse, ((1,), (1,)))


def step_kernel(place_ref, *refs):
    tm_size = step_kernel.tm_size
    panel_size = step_kernel.panel_size
    received = refs[:tm_size]
    split_ref, work_ref, current_ref, product_ref = refs[tm_size : tm_size + 4]
    next_ref, next_product_ref, next_work_ref, packed_ref, gram_ref, diagonal_ref, upper_ref = refs[
        tm_size + 4 : tm_size + 11
    ]
    pairs_ref, high_ref, low_ref, total_ref, result_ref = refs[tm_size + 11 :]
    rows, n = work_ref.shape
    half = rows // 2
    channels = split_ref.shape[0] // 2
    lags_here = rows // channels
    pair_count = (lags_here + 1) // 2
    front = 2 * pair_count * channels
    length = split_ref.shape[1]
    data = tm_size * panel_size * rows

    pairs_ref[: front + channels, :] = jnp.zeros((front + channels, 2 * n), f32)
    tail = pairs_ref.shape[0] - (front + data)
    pairs_ref[front + data :, :] = jnp.zeros((tail, 2 * n), f32)
    for step in range(tm_size):
        origin = lax.rem(place_ref[0] + tm_size - step, tm_size) * panel_size

        def unpack(p, carry, step=step, origin=origin):
            source = lax.rem(place_ref[1] + panel_size - p, panel_size)
            to = pl.multiple_of(front + (origin + source) * rows, 8)
            value = received[step][pl.ds(pl.multiple_of(p * half, 8), half), :]
            swapped = pltpu.roll(value, n, 1)
            pairs_ref[pl.ds(to, half), :n] = value[:, :n]
            pairs_ref[pl.ds(to + half, half), :n] = swapped[:, :n]
            pairs_ref[pl.ds(to + channels, half), n:] = swapped[:, n:]
            pairs_ref[pl.ds(to + channels + half, half), n:] = value[:, n:]
            return carry

        lax.fori_loop(0, panel_size, unpack, 0)

    def halves(c, carry):
        at = pl.ds(pl.multiple_of(c * 96, 32), 96)
        value = pairs_ref[at, :]
        upper_half = value.astype(bf16)
        high_ref[at, :] = upper_half
        low_ref[at, :] = (value - upper_half.astype(f32)).astype(bf16)
        return carry

    lax.fori_loop(0, pairs_ref.shape[0] // 96, halves, 0)

    total_ref[...] = jnp.zeros(total_ref.shape, f32)

    def multiply(c, carry):
        first = c * K_STEP
        left = split_ref[:, pl.ds(pl.multiple_of(first, 128), K_STEP)]
        for pair in range(0, pair_count, 2):
            group = range(pair, min(pair + 2, pair_count))
            at = [pl.ds(pl.multiple_of(first + front - 2 * channels * j, 16), K_STEP) for j in group]
            high = jnp.concatenate([high_ref[s, :] for s in at], axis=1)
            low = jnp.concatenate([low_ref[s, :] for s in at], axis=1)
            lanes = slice(pair * 2 * n, (pair + len(group)) * 2 * n)
            first_part = fast_dot(left, high)
            second_part = fast_dot(left[:channels], low)
            total_ref[:, lanes] += first_part[:channels] + (first_part[channels:] + second_part)
        return carry

    lax.fori_loop(0, length // K_STEP, multiply, 0)
    for shift in range(lags_here):
        at = (lags_here - 1 - shift) * channels
        next_product_ref[at : at + channels, :] = total_ref[:, shift * n : (shift + 1) * n]

    gram = received[0][panel_size * half :, :]
    for step in range(1, tm_size):
        gram = gram + received[step][panel_size * half :, :]
    current = current_ref[...]
    diagonal, upper, inverse, following = orthogonalize(gram, work_ref[...], current, result_ref)
    product = next_product_ref[...] - exact_dot(product_ref[...], diagonal)
    product = exact_dot(product, inverse, ((1,), (1,)))
    work = product - exact_dot(current, upper, ((1,), (1,)))
    diagonal_ref[...] = diagonal
    upper_ref[...] = upper
    next_ref[...] = following
    next_product_ref[...] = product
    next_work_ref[...] = work
    packed_ref[:, :n] = work[:half]
    packed_ref[:, n:] = work[half:]
    together = jnp.concatenate([following, work], axis=1)
    gram_ref[...] = exact_dot(together, together, ((0,), (0,)))


def last_kernel(*refs):
    received = refs[:-7]
    work_ref, current_ref, next_ref, diagonal_ref, upper_ref, result_ref = refs[-6:]
    gram = refs[-7][...]
    for other in received:
        gram = gram + other[...]
    diagonal, upper, _, following = orthogonalize(gram, work_ref[...], current_ref[...], result_ref)
    diagonal_ref[...] = diagonal
    upper_ref[...] = upper
    next_ref[...] = following


def lanczos_step(place, received, split, work, current, product):
    rows, n = work.shape
    channels = split.shape[0] // 2
    pair_count = (rows // channels + 1) // 2
    front = 2 * pair_count * channels
    depth = front + split.shape[1] + 2 * channels
    depth = -(-depth // 96) * 96
    step_kernel.tm_size = lax.axis_size("tm")
    step_kernel.panel_size = lax.axis_size("panel")
    tall = jax.ShapeDtypeStruct((rows, n), f32)
    small = jax.ShapeDtypeStruct((n, n), f32)
    vmem = pl.BlockSpec(memory_space=pltpu.VMEM)
    return pl.pallas_call(
        step_kernel,
        in_specs=[pl.BlockSpec(memory_space=pltpu.SMEM)] + [vmem] * (len(received) + 4),
        out_shape=(
            tall,
            tall,
            tall,
            jax.ShapeDtypeStruct((rows // 2, 2 * n), f32),
            jax.ShapeDtypeStruct((2 * n, 2 * n), f32),
            small,
            small,
        ),
        scratch_shapes=[
            pltpu.VMEM((depth, 2 * n), f32),
            pltpu.VMEM((depth, 2 * n), bf16),
            pltpu.VMEM((depth, 2 * n), bf16),
            pltpu.VMEM((channels, pair_count * 2 * n), f32),
            pltpu.VMEM((n, 2 * n), f32),
        ],
        name="lanczos_step",
    )(place, *received, split, work, current, product)


def last_step(received, work, current):
    n = work.shape[1]
    small = jax.ShapeDtypeStruct((n, n), f32)
    return pl.pallas_call(
        last_kernel,
        out_shape=(jax.ShapeDtypeStruct(work.shape, f32), small, small),
        scratch_shapes=[pltpu.VMEM((n, 2 * n), f32)],
        name="last_step",
    )(*received, work, current)


def exchanged(packed, gram):
    half = packed.shape[0]
    near = shifted_around(jnp.concatenate([packed, gram], axis=0), "panel")
    gram = sum(piece[half:] for piece in near[1:]) + near[0][half:]
    group = jnp.concatenate([piece[:half] for piece in near] + [gram], axis=0)
    return shifted_around(group, "tm")


def local(series, start_block):
    channels, days_here = series.shape
    rows, n = start_block.shape
    tm_size = lax.axis_size("tm")
    tm_at = lax.axis_index("tm")
    panel_at = lax.axis_index("panel")
    lags_here = rows // channels
    block_index = tm_at * lax.axis_size("panel") + panel_at

    packed = jnp.concatenate([start_block[: rows // 2], start_block[rows // 2 :]], axis=1)
    start_gram = exact_dot(start_block, start_block, ((0,), (0,)))
    gram = jnp.pad(start_gram, ((n, 0), (n, 0)))

    pieces = shifted_around(series, "tm")
    twice = jnp.concatenate(pieces[::-1] + pieces[::-1], axis=1)
    first = (tm_size - 1 - tm_at) * days_here
    whole = lax.dynamic_slice(twice, (jnp.int32(0), first), (channels, tm_size * days_here))
    window, split = lag_window(whole, block_index, lags_here)
    covariance = covariance_rows(window, lags_here)

    place = jnp.stack([tm_at, panel_at]).astype(jnp.int32)
    work = start_block
    current = jnp.zeros_like(work)
    product = jnp.zeros_like(work)
    basis_list, diagonal_list, upper_list = [], [], []
    for _ in range(ITERS):
        received = exchanged(packed, gram)
        current, product, work, packed, gram, diagonal, upper = lanczos_step(
            place, received, split, work, current, product
        )
        basis_list.append(current)
        diagonal_list.append(diagonal)
        upper_list.append(upper)
    near = shifted_around(gram, "panel")
    grams = shifted_around(sum(near[1:]) + near[0], "tm")
    current, diagonal, upper = last_step(grams, work, current)
    basis_list.append(current)
    diagonal_list.append(diagonal)
    upper_list.append(upper)
    return (
        covariance,
        jnp.stack(basis_list),
        jnp.stack(diagonal_list[1:]),
        jnp.stack(upper_list),
    )


def solution(mesh):
    placed = (P(None, "tm"), P(("tm", "panel"), None))
    return jax.shard_map(
        local,
        mesh=mesh,
        in_specs=placed,
        out_specs=(P(("tm", "panel"), None), P(None, ("tm", "panel"), None), P(), P()),
        check_vma=False,
    )
```
